32 devices in a mesh: island: 4 (over y, core), section: 4 (over z), tensor: 2 (over x).
Axes of the slice: x: 2, y: 2, z: 4, core: 2. Of those that a mesh axis runs over, the one named last changes fastest.
Arguments:
- hidden: bfloat16 [4, 4, 256, 8192], P('island', 'section', 'tensor'), may hold values from -6 to 6
- norm_gain: bfloat16 [4, 8192], P('section'), may hold values from 0.099609375 to 1.8984375
- grad_above: bfloat16 [4, 256, 8192], P('island', 'tensor'), may hold values from -6 to 6
- key_cot: bfloat16 [4, 4, 256, 1024], P('island', 'section', None, 'tensor'), may hold values from -6 to 6
- value_cot: bfloat16 [4, 4, 256, 1024], P('island', 'section', None, 'tensor'), may hold values from -6 to 6
- local_key: bfloat16 [4, 4, 8192, 1024], P('island', 'section', None, 'tensor'), may hold values from -6 to 6
- local_value: bfloat16 [4, 4, 8192, 1024], P('island', 'section', None, 'tensor'), may hold values from -6 to 6
- anchor_key: float32 [4, 8192, 1024], P('section', 'island', 'tensor'), may hold values from -6 to 6
- anchor_value: float32 [4, 8192, 1024], P('section', 'island', 'tensor'), may hold values from -6 to 6
- momentum_key: float32 [4, 8192, 1024], P('section', 'island', 'tensor'), may hold values from -4 to 4
- momentum_value: float32 [4, 8192, 1024], P('section', 'island', 'tensor'), may hold values from -4 to 4
Outputs:
- anchor_key_new: float32 [4, 8192, 1024], P('section', 'island', 'tensor')
- anchor_value_new: float32 [4, 8192, 1024], P('section', 'island', 'tensor')
- momentum_key_new: float32 [4, 8192, 1024], P('section', 'island', 'tensor')
- momentum_value_new: float32 [4, 8192, 1024], P('section', 'island', 'tensor')
- input_grad: bfloat16 [4, 4, 256, 8192], P('island', 'section', 'tensor')
The draws below stay inside these ranges and needn't reach their ends.
All inputs are finite; a program needn't handle non-finite values.
Results may differ from the reference program's by a relative error of at most 0.024.
Values may be sent and summed in bfloat16 or wider, within the bound.
No kernel may reach another device: no remote copies, remote signals or barrier semaphores. Data moves between devices by JAX's collectives and lax.ppermute only.
A program may use at most 128 MiB of HBM per device.

```python
import jax
import jax.numpy as jnp
from jax import lax

D = 8192
TOK = 256
KV = 1024
ISLANDS = 4
SECTIONS = 4
N_ISLAND = 4
N_SECTION = 4
N_TENSOR = 2


def raised(entries, stream_key, source, target, shards_of, factor):
    owner, partner = [(jnp.arange(entries.shape[dim]) // (entries.shape[dim] // shards_of)).reshape([-1 if axis == dim else 1 for axis in range(entries.ndim)]) for dim in (source, target)]
    chosen = jax.random.permutation(stream_key, shards_of)[partner]
    strong = (owner == chosen) | (owner == (partner + shards_of // 2) % shards_of)
    return jnp.where(strong, factor * entries, entries)


def steps_of(rng, dims, cuts, smallest, top_value):
    factor_of, own = 1.0, jax.random.fold_in(rng, 6)
    for axis_at, shards_of in cuts:
        heights = jnp.exp(jax.random.uniform(jax.random.fold_in(own, axis_at), (shards_of,), jnp.float32, smallest / len(cuts), top_value / len(cuts)))
        factor_of = factor_of * jnp.repeat(heights, dims[axis_at] // shards_of).reshape([-1 if axis == axis_at else 1 for axis in range(len(dims))])
    return factor_of


def centred(key, dims, spread, reach, shards=(), kind=jnp.bfloat16):
    values = jax.random.normal(key, dims, jnp.float32) * spread
    if len(shards) > 0:
        values = steps_of(key, dims, shards, -0.22, 0.18) * values
    return jnp.clip(values, min=-reach, max=reach).astype(kind)


def gaussian_with(stream_key, dims, scale, most, pieces, heavy, kind=jnp.bfloat16):
    result = scale * jax.random.normal(stream_key, dims, jnp.float32)
    if pieces:
        result = result * steps_of(stream_key, dims, pieces, -0.22, 0.18)
    return jnp.clip(raised(result, jax.random.fold_in(stream_key, 3), *heavy), -most, most).astype(kind)


def setup_inputs(seed: int = 0) -> dict:
    splits = jax.random.split(jax.random.key(seed), 12)
    hidden = centred(splits[0], (ISLANDS, SECTIONS, TOK, D), 1.0, 6.0, ((0, 4), (1, 4), (2, 2)))
    norm_gain = jnp.clip(1.0 + 0.18 * jax.random.normal(splits[1], (SECTIONS, D), jnp.float32), 0.099609375, 1.8984375).astype(jnp.bfloat16)
    grad_above = centred(splits[2], (ISLANDS, TOK, D), 1.0, 6.0, ((0, 4), (1, 2)))
    key_cot = centred(splits[3], (ISLANDS, SECTIONS, TOK, KV), 1.0, 6.0, ((0, 4), (1, 4), (3, 2)))
    value_cot = centred(splits[4], (ISLANDS, SECTIONS, TOK, KV), 1.0, 6.0, ((0, 4), (1, 4), (3, 2)))
    local_key = gaussian_with(splits[5], (ISLANDS, SECTIONS, D, KV), 1.0, 6.0, ((0, 4), (1, 4), (3, 2)), (0, 2, 4, 2.0))
    local_value = gaussian_with(splits[6], (ISLANDS, SECTIONS, D, KV), 1.0, 6.0, ((0, 4), (1, 4), (3, 2)), (0, 2, 4, 2.0))
    anchor_key = centred(splits[7], (SECTIONS, D, KV), 1.0, 6.0, ((0, 4), (1, 4), (2, 2)), jnp.float32)
    anchor_value = centred(splits[8], (SECTIONS, D, KV), 1.0, 6.0, ((0, 4), (1, 4), (2, 2)), jnp.float32)
    momentum_key = centred(splits[9], (SECTIONS, D, KV), 0.5, 4.0, ((0, 4), (1, 4), (2, 2)), jnp.float32)
    momentum_value = centred(splits[10], (SECTIONS, D, KV), 0.5, 4.0, ((0, 4), (1, 4), (2, 2)), jnp.float32)
    return dict(hidden=hidden, norm_gain=norm_gain, grad_above=grad_above, key_cot=key_cot, value_cot=value_cot, local_key=local_key, local_value=local_value, anchor_key=anchor_key, anchor_value=anchor_value, momentum_key=momentum_key, momentum_value=momentum_value)


epsilon = 1e-05
inner_rate = 0.5
outer_rate = 0.7
outer_beta = 0.9

def norm_parts(resid, gains):
    inverse_rms = lax.rsqrt(lax.optimization_barrier(jnp.mean(resid * resid, axis=-1, keepdims=True)) + epsilon)
    normed = (resid * inverse_rms * gains).astype(jnp.bfloat16)
    return (inverse_rms, normed)

def norm_backward(resid, inverse_rms, gains, upstream):
    scaled = gains * upstream
    return inverse_rms * scaled - resid * inverse_rms ** 3 * lax.optimization_barrier(jnp.mean(resid * scaled, axis=-1, keepdims=True))

def contract_rows(left, right):
    return lax.dot_general(left, right, (((0,), (0,)), ((), ())), preferred_element_type=jnp.float32)

def contract_cols(left, right):
    return lax.dot_general(left, right, (((1,), (1,)), ((), ())), preferred_element_type=jnp.float32)

def outer_update(anchor, momentum, mean_delta):
    momentum_new = outer_beta * momentum + mean_delta
    return (anchor - outer_rate * (mean_delta + outer_beta * momentum_new), momentum_new)

def reference(hidden, norm_gain, grad_above, key_cot, value_cot, local_key, local_value, anchor_key, anchor_value, momentum_key, momentum_value):
    factor = float(D) ** (-0.5)
    width = KV // N_TENSOR
    key_sums = [jnp.zeros((D, KV), jnp.float32) for section_index in range(N_SECTION)]
    value_sums = [jnp.zeros((D, KV), jnp.float32) for section_index in range(N_SECTION)]
    grads_out = []
    for island in range(N_ISLAND):
        branches = []
        for section_index in range(N_SECTION):
            resid = hidden[island, section_index].astype(jnp.float32)
            gains = norm_gain[section_index].astype(jnp.float32)
            inverse_rms, normed = norm_parts(resid, gains)
            key_rows = key_cot[island, section_index]
            value_rows = value_cot[island, section_index]
            weight_key = local_key[island, section_index]
            weight_value = local_value[island, section_index]
            grad_key = contract_rows(normed, key_rows) * factor
            grad_value = contract_rows(normed, value_rows) * factor
            new_key = weight_key.astype(jnp.float32) - inner_rate * grad_key
            new_value = weight_value.astype(jnp.float32) - inner_rate * grad_value
            key_sums[section_index] = key_sums[section_index] + (anchor_key[section_index] - new_key)
            value_sums[section_index] = value_sums[section_index] + (anchor_value[section_index] - new_value)
            upstream = jnp.zeros((TOK, D), jnp.float32)
            for member in range(N_TENSOR):
                low = member * width
                high = low + width
                partial_value = (contract_cols(key_rows[:, low:high], weight_key[:, low:high]) + contract_cols(value_rows[:, low:high], weight_value[:, low:high])) * factor
                rounded = lax.optimization_barrier(partial_value.astype(jnp.bfloat16))
                upstream = upstream + rounded.astype(jnp.float32)
            branches.append(norm_backward(resid, inverse_rms, gains, upstream))
        running = grad_above[island].astype(jnp.float32)
        section_grads = [None] * N_SECTION
        for section_index in range(N_SECTION - 1, -1, -1):
            running = running + branches[section_index]
            section_grads[section_index] = running.astype(jnp.bfloat16)
        grads_out.append(jnp.stack(section_grads))
    input_grad = jnp.stack(grads_out)
    anchors_key, moments_key, anchors_value, moments_value = ([], [], [], [])
    for section_index in range(N_SECTION):
        new_anchor, new_moment = outer_update(anchor_key[section_index], momentum_key[section_index], key_sums[section_index] / N_ISLAND)
        anchors_key.append(new_anchor)
        moments_key.append(new_moment)
        new_anchor, new_moment = outer_update(anchor_value[section_index], momentum_value[section_index], value_sums[section_index] / N_ISLAND)
        anchors_value.append(new_anchor)
        moments_value.append(new_moment)
    return (jnp.stack(anchors_key), jnp.stack(anchors_value), jnp.stack(moments_key), jnp.stack(moments_value), input_grad)
```

```python
import jax
import jax.numpy as jnp
from jax import lax
from jax.experimental import pallas as pl
from jax.experimental.pallas import tpu as pltpu
from jax.sharding import PartitionSpec as P

epsilon = 1e-05
inner_rate = 0.5
outer_rate = 0.7
outer_beta = 0.9


f32 = jnp.float32
bf16 = jnp.bfloat16
VMEM_LIMIT = 48 * 1024 * 1024


def spec(shape, index):
    return pl.BlockSpec(shape, index)


def call(body, grid, scalars, in_specs, out_specs, out_shape, operands, flops, aliases=None):
    moved = sum(a.size * a.dtype.itemsize for a in operands)
    moved += sum(s.size * s.dtype.itemsize for s in jax.tree.leaves(out_shape))
    return pl.pallas_call(
        body,
        grid_spec=pltpu.PrefetchScalarGridSpec(
            num_scalar_prefetch=1, grid=grid, in_specs=in_specs, out_specs=out_specs
        ),
        out_shape=out_shape,
        input_output_aliases={} if aliases is None else aliases,
        compiler_params=pltpu.CompilerParams(
            dimension_semantics=("arbitrary",) * len(grid), vmem_limit_bytes=VMEM_LIMIT
        ),
        cost_estimate=pl.CostEstimate(flops=flops, bytes_accessed=moved, transcendentals=0),
    )(scalars, *operands)


def shape(dims, kind):
    return jax.ShapeDtypeStruct(dims, kind)


def contract_rows(left, right):
    return lax.dot_general(left, right, (((0,), (0,)), ((), ())), preferred_element_type=f32)


def contract_cols(left, right):
    return lax.dot_general(left, right, (((1,), (1,)), ((), ())), preferred_element_type=f32)


def norm_kernel(island, hidden, gain, cores, chunk):
    tokens, features = hidden.shape
    outer = features // chunk // cores
    rows = min(tokens, 16)

    def body(i_ref, h_ref, g_ref, keep_ref, give_ref, inv_ref):
        core = lax.rem(i_ref[0], cores)
        resid = h_ref[...].astype(f32)
        inv = lax.rsqrt(jnp.mean(resid * resid, axis=-1, keepdims=True) + epsilon)
        inv_ref[...] = inv
        for o in range(outer):
            for ref, which in ((keep_ref, core), (give_ref, 1 - core)):
                at = pl.ds(pl.multiple_of((cores * o + which) * chunk, chunk), chunk)
                ref[:, o * chunk : (o + 1) * chunk] = (
                    h_ref[:, at].astype(f32) * inv * g_ref[:, at].astype(f32)
                ).astype(bf16)

    half = features // cores
    return call(
        body,
        (tokens // rows,),
        island,
        [spec((rows, features), lambda g, i: (g, 0)), spec((1, features), lambda g, i: (0, 0))],
        [
            spec((rows, half), lambda g, i: (g, 0)),
            spec((rows, half), lambda g, i: (g, 0)),
            spec((rows, 1), lambda g, i: (g, 0)),
        ],
        [shape((tokens, half), bf16), shape((tokens, half), bf16), shape((tokens, 1), f32)],
        [hidden, gain],
        4 * tokens * features,
    )


def partial_kernel(island, cots, weight_key, weight_value, groups, factor):
    tokens, both = cots.shape
    features, columns = weight_key.shape
    tile = min(features, 512)

    def body(i_ref, c_ref, k_ref, v_ref, *out_refs):
        part = contract_cols(c_ref[:, :columns], k_ref[...])
        part += contract_cols(c_ref[:, columns:], v_ref[...])
        part = (part * factor).astype(bf16)
        low = 0
        for ref, size in zip(out_refs, groups):
            ref[...] = part[low : low + size]
            low += size

    return call(
        body,
        (features // tile,),
        island,
        [
            spec((tokens, both), lambda g, i: (0, 0)),
            spec((tile, columns), lambda g, i: (g, 0)),
            spec((tile, columns), lambda g, i: (g, 0)),
        ],
        [spec((size, tile), lambda g, i: (0, g)) for size in groups],
        [shape((size, features), bf16) for size in groups],
        [cots, weight_key, weight_value],
        2 * tokens * features * both,
    )


class Rows:
    def __init__(self, cores, outers, chunk, tile, turn, start):
        self.cores, self.outers, self.per, self.turn, self.first = (
            cores,
            outers,
            chunk // tile,
            turn,
            start // tile,
        )

    def outer(self, i):
        return lax.rem(i[0] // self.cores + self.turn, self.outers)

    def of_weights(self, g, i):
        core = lax.rem(i[0], self.cores)
        return (self.outer(i) * self.cores + core) * self.per + self.first + g

    def of_half(self, g, i):
        return self.outer(i) * self.per + self.first + g


def product(mine, theirs, cots):
    total, low = None, 0
    for block in mine + theirs:
        high = low + block.shape[0]
        part = contract_rows(block[...], cots[low:high])
        total = part if total is None else total + part
        low = high
    return total


def delta_specs(rows, first, tile, pair, remote, cots, columns):
    specs = [spec((p.shape[0], tile), lambda g, i: (0, rows.of_half(g, i))) for p in pair]
    specs += [spec((p.shape[0], tile), lambda g, i: (0, first + g)) for p in remote]
    specs += [spec(cots.shape, lambda g, i: (0, 0))]
    specs += [spec((tile, columns), lambda g, i: (rows.of_weights(g, i), 0))] * 2
    return specs


def send_kernel(island, rows, count, tile, pair, remote, cots, weights, got, rate):
    columns = weights[0].shape[1]
    n_pair, n_all = len(pair), len(pair) + len(remote)
    per = rows.first

    def body(i_ref, *refs):
        parts = product(list(refs[:n_pair]), list(refs[n_pair:n_all]), refs[n_all])
        wk, wv, got_ref, out_ref = refs[n_all + 1 :]
        for at, w in ((0, wk), (1, wv)):
            low = at * columns
            base = w[...].astype(f32) + got_ref[at].astype(f32)
            out_ref[:, low : low + columns] = (
                base - rate * parts[:, low : low + columns]
            ).astype(bf16)

    return call(
        body,
        (count // tile,),
        island,
        delta_specs(rows, 0, tile, pair, remote, cots, columns)
        + [spec((2, tile, columns), lambda g, i: (0, per + g, 0))],
        spec((tile, 2 * columns), lambda g, i: (g, 0)),
        shape((count, 2 * columns), bf16),
        [*pair, *remote, cots, *weights, got],
        2 * count * cots.shape[0] * 2 * columns,
    )


def update_kernel(
    island, rows, count, tile, pair, remote, first, cots, weights, got, arrived, state, done, rate, islands
):
    columns = weights[0].shape[1]
    n_pair, n_all = len(pair), len(pair) + len(remote)
    n_in = n_all + 4 + len(arrived) + 4
    per = rows.first
    n_done = 0 if done is None else 4

    def body(i_ref, *refs):
        parts = product(list(refs[:n_pair]), list(refs[n_pair:n_all]), refs[n_all])
        weight_refs, got_ref = refs[n_all + 1 : n_all + 3], refs[n_all + 3]
        come = refs[n_all + 4 : n_all + 4 + len(arrived)]
        anchors = refs[n_in - 4 : n_in - 2]
        momenta = refs[n_in - 2 : n_in]
        outs = refs[n_in + n_done :]
        for at in range(2):
            low = at * columns
            total = weight_refs[at][...].astype(f32) + got_ref[at].astype(f32)
            total -= rate * parts[:, low : low + columns]
            for ref in come:
                total += ref[:, low : low + columns].astype(f32)
            anchor = anchors[at][...]
            mean = anchor - total / islands
            momentum = outer_beta * momenta[at][...] + mean
            outs[at][...] = anchor - outer_rate * (mean + outer_beta * momentum)
            outs[2 + at][...] = momentum

    whole = state[0].shape
    own = spec((tile, columns), lambda g, i: (per + g, 0))
    specs = (
        delta_specs(rows, first // tile, tile, pair, remote, cots, columns)
        + [spec((2, tile, columns), lambda g, i: (0, per + g, 0))]
        + [spec((tile, 2 * columns), lambda g, i: (g, 0))] * len(arrived)
        + [own] * 4
    )
    operands = [*pair, *remote, cots, *weights, got, *arrived, *state]
    aliases = {}
    if done is not None:
        specs += [pl.BlockSpec(memory_space=pl.ANY)] * 4
        aliases = {1 + len(operands) + k: k for k in range(4)}
        operands += list(done)
    return call(
        body,
        (count // tile,),
        island,
        specs,
        [own] * 4,
        [shape(whole, f32)] * 4,
        operands,
        2 * count * cots.shape[0] * 2 * columns,
        aliases,
    )


def branch_kernel(start, count, hidden, gain, inv, own, parts, above, top):
    features = hidden.shape[1]
    rows = min(count, 16)
    base = start // rows
    n_parts = len(parts)

    def body(t_ref, h_ref, g_ref, inv_ref, own_ref, *refs):
        above_ref, out_ref, out16_ref = refs[n_parts:]
        upstream = own_ref[...].astype(f32)
        for ref in refs[:n_parts]:
            upstream += ref[...].astype(f32)
        scaled = g_ref[...].astype(f32) * upstream
        resid = h_ref[...].astype(f32)
        inv_rms = inv_ref[...]
        mean = jnp.mean(resid * scaled, axis=-1, keepdims=True)
        is_top = (t_ref[0] == 1).astype(f32)
        term = inv_rms * scaled - resid * (inv_rms * inv_rms * inv_rms * mean)
        term += is_top * above_ref[...].astype(f32)
        out_ref[...] = term
        out16_ref[...] = term.astype(bf16)

    own_rows = spec((rows, features), lambda g, i: (base + g, 0))
    part_rows = spec((rows, features), lambda g, i: (g, 0))
    return call(
        body,
        (count // rows,),
        top,
        [
            own_rows,
            spec((1, features), lambda g, i: (0, 0)),
            spec((rows, 1), lambda g, i: (base + g, 0)),
            own_rows,
            *[part_rows] * n_parts,
            own_rows,
        ],
        [part_rows, part_rows],
        [shape((count, features), f32), shape((count, features), bf16)],
        [hidden, gain, inv, own, *parts, above],
        8 * count * features,
    )


def final_kernel(island, start, tokens, term, arrived, done):
    count, features = term.shape
    rows = min(count, 16)
    base = start // rows

    def body(i_ref, term_ref, *refs):
        total = term_ref[...]
        for ref in refs[: len(arrived)]:
            total += ref[...].astype(f32)
        refs[-1][...] = total.astype(bf16)

    part_rows = spec((rows, features), lambda g, i: (g, 0))
    specs = [part_rows] * (1 + len(arrived))
    operands = [term, *arrived]
    aliases = {}
    if done is not None:
        specs.append(pl.BlockSpec(memory_space=pl.ANY))
        aliases = {1 + len(operands): 0}
        operands.append(done)
    return call(
        body,
        (count // rows,),
        island,
        specs,
        spec((rows, features), lambda g, i: (base + g, 0)),
        shape((tokens, features), bf16),
        operands,
        4 * count * features,
        aliases,
    )


def move(block, axis, target):
    size = lax.axis_size(axis)
    route = [(i, target(i)) for i in range(size) if target(i) is not None]
    return lax.ppermute(block, axis, route)


def local(
    hidden,
    norm_gain,
    grad_above,
    key_cot,
    value_cot,
    local_key,
    local_value,
    anchor_key,
    anchor_value,
    momentum_key,
    momentum_value,
):
    islands, sections, tensors = (lax.axis_size(a) for a in ("island", "section", "tensor"))
    cores = 2
    outers = islands // cores
    island = lax.axis_index("island")
    section = lax.axis_index("section")
    tensor = lax.axis_index("tensor")
    core, outer = island % cores, island // cores
    scalars = island.astype(jnp.int32).reshape(1)
    top = (section == sections - 1).astype(jnp.int32).reshape(1)

    resid, above = hidden[0, 0], grad_above[0]
    weights = [local_key[0, 0], local_value[0, 0]]
    tokens, features = resid.shape
    columns = weights[0].shape[1]
    factor = float(features) ** (-0.5)
    owned = features // islands
    state = [a[0] for a in (anchor_key, anchor_value, momentum_key, momentum_value)]

    def across(i):
        return i - i % cores + (cores - 1 - i % cores)

    cot = jnp.concatenate([key_cot[0, 0], value_cot[0, 0]], axis=1)
    cot = cot.reshape(tensors, tokens, 2 * columns)
    cots = jnp.concatenate(
        [
            lax.dynamic_index_in_dim(cot, (tensor + e) % tensors, 0, keepdims=False)
            for e in range(tensors)
        ]
    )
    cots_other = move(cots, "island", across)
    order = []
    for e in range(tensors):
        for c in (cots, cots_other):
            order.append(c[e * tokens : (e + 1) * tokens])
    all_cots = jnp.concatenate(order)

    got = []
    for turn in list(range(1, outers)) + [0]:
        block = jnp.stack(
            [
                lax.dynamic_slice_in_dim(
                    w,
                    (((outer + turn) % outers) * cores + (cores - 1 - core)) * owned,
                    owned,
                )
                for w in weights
            ]
        )
        got.append(move(block, "island", across))
    got = [got[-1], *got[:-1]]

    keep, give, inv = norm_kernel(scalars, resid, norm_gain, cores, owned)
    other = move(give, "island", across)
    pair = [keep, other]

    n_rows = 4
    n_tokens = max(1, min(4, tokens // 16))
    row_chunk, token_chunk = owned // n_rows, tokens // n_tokens

    def gather(turn, start, count):
        low = ((outer + turn) % outers) * owned + start
        block = jnp.concatenate([lax.dynamic_slice_in_dim(p, low, count, axis=1) for p in pair])
        come = []
        for e in range(1, tensors):
            come.append(move(block, "tensor", lambda i: (i - e) % tensors))
        return come

    groups = [tokens] + [token_chunk] * (n_tokens * (tensors - 1))
    partials = partial_kernel(scalars, cots, *weights, groups, factor)
    own_part, parts = partials[0], partials[1:]
    tile = min(row_chunk, 256)

    sent = {}
    for q in range(n_rows):
        for turn in range(1, outers):
            remote = gather(turn, q * row_chunk, row_chunk)
            rows = Rows(cores, outers, owned, tile, turn, q * row_chunk)
            block = send_kernel(
                scalars,
                rows,
                row_chunk,
                tile,
                pair,
                remote,
                all_cots,
                weights,
                got[turn],
                inner_rate * factor,
            )
            sent[q, turn] = move(
                block, "island", lambda i: (i + turn * cores) % islands
            )

    input_grad = None
    for q in range(n_tokens):
        arrived = []
        for e in range(1, tensors):
            arrived.append(
                move(
                    parts[(e - 1) * n_tokens + q],
                    "tensor",
                    lambda i: (i + e) % tensors,
                )
            )
        term, rounded = branch_kernel(
            q * token_chunk, token_chunk, resid, norm_gain, inv, own_part, arrived, above, top
        )
        hops = []
        for hop in range(sections - 1):
            if hop:
                running = term
                for come in hops:
                    running = running + come.astype(f32)
                rounded = running.astype(bf16)
            hops.append(
                move(
                    rounded,
                    "section",
                    lambda i: i - 1 if i == sections - 1 - hop else None,
                )
            )
        input_grad = final_kernel(scalars, q * token_chunk, tokens, term, hops, input_grad)

    outs = None
    n_own = 2
    own_chunk = owned // n_own
    for q in range(n_rows):
        if q % (n_rows // n_own) == 0:
            remote = gather(0, q * row_chunk, own_chunk)
        rows = Rows(cores, outers, owned, tile, 0, q * row_chunk)
        outs = update_kernel(
            scalars,
            rows,
            row_chunk,
            tile,
            pair,
            remote,
            (q % (n_rows // n_own)) * row_chunk,
            all_cots,
            weights,
            got[0],
            [sent[q, turn] for turn in range(1, outers)],
            state,
            outs,
            inner_rate * factor,
            islands,
        )
    return (*[o[None] for o in outs], input_grad[None, None])


def solution(mesh):
    placed = (
        P("island", "section", "tensor", None),
        P("section", None),
        P("island", "tensor", None),
        P("island", "section", None, "tensor"),
        P("island", "section", None, "tensor"),
        P("island", "section", None, "tensor"),
        P("island", "section", None, "tensor"),
        P("section", "island", "tensor"),
        P("section", "island", "tensor"),
        P("section", "island", "tensor"),
        P("section", "island", "tensor"),
    )

    return jax.shard_map(
        local,
        mesh=mesh,
        in_specs=placed,
        out_specs=(
            P("section", "island", "tensor"),
            P("section", "island", "tensor"),
            P("section", "island", "tensor"),
            P("section", "island", "tensor"),
            P("island", "section", "tensor", None),
        ),
        check_vma=False,
    )
```
